256 devices in a mesh: seq: 64 (over z, y, core), mp: 4 (over x).
Axes of the slice: x: 4, y: 4, z: 8, core: 2. Of those that a mesh axis runs over, the one named last changes fastest.
Arguments:
- queries: bfloat16 [131072, 4096], P('seq', 'mp'), may hold values from -1000 to 1000, as said below
- encoded: bfloat16 [256, 32, 896], P('seq'), may hold values from -6 to 6
- w_kv: bfloat16 [896, 2, 4096], P(None, None, 'mp'), may hold values from -0.1875 to 0.1875
- retrieved: int32 [2048, 2], P('seq'), may hold values from 0 to 255, as said below
Outputs:
- attended: bfloat16 [131072, 4096], P('seq', 'mp')
The draws below stay inside these ranges and needn't reach their ends.
Inputs may be any that keep to these rules, and one draw needn't show every extreme that they name: Decoder queries; their rows have unequal scales. `retrieved`: tile i is stored on index i // 4 of seq; of the 64 ids of one index of seq, exactly 1 name tiles stored on each index of seq; a tile may be named by many groups.
All inputs are finite; a program needn't handle non-finite values.
Results may differ from the reference program's by a relative error of at most 0.012.
Values may be sent and summed in bfloat16 or wider, within the bound.
A program may use at most 128 MiB of HBM per device.

```python
import math
import jax
import jax.numpy as jnp
from jax import lax

D = 4096
HEADS = 32
D_ENC = 896
GROUP = 64
R = 32
CH_DEV = 32
HEAD_DIM = 128
GROUPS = 2048
TOKENS = 131072
NB_DEV = 4
NBR = 256


def draw_queries(key, part):
    key_base, key_scale = jax.random.split(key, 2)
    base = jnp.clip(jax.random.normal(key_base, (TOKENS, D), jnp.float32), -6.0, 6.0)
    row_scale = jnp.exp(jax.random.uniform(key_scale, (TOKENS, 1), jnp.float32, 0.0, math.log(3.0)))
    return (base * row_scale).astype(jnp.bfloat16)


def draw_retrieved(key, part):
    devices = GROUPS // CH_DEV
    ref_count = 2 * CH_DEV
    key_order, key_first, key_second = jax.random.split(key, 3)
    ref_order = jax.vmap(lambda one_key: jax.random.permutation(one_key, ref_count))(jax.random.split(key_order, devices))
    owners = ref_order % devices
    first = jax.random.randint(key_first, (devices, ref_count), 0, NB_DEV)
    second = jax.random.randint(key_second, (devices, ref_count), 0, NB_DEV)
    local_ids = first * second // NB_DEV
    tile_ids = owners * NB_DEV + local_ids
    return tile_ids.reshape(GROUPS, 2).astype(jnp.int32)


def levels(rng, dims, pieces, smallest, top_value):
    factor_of, own = 1.0, jax.random.fold_in(rng, 6)
    for axis_at, shards_of in pieces:
        heights = jnp.exp(jax.random.uniform(jax.random.fold_in(own, axis_at), (shards_of,), jnp.float32, smallest / len(pieces), top_value / len(pieces)))
        factor_of = factor_of * jnp.repeat(heights, dims[axis_at] // shards_of).reshape([-1 if axis == axis_at else 1 for axis in range(len(dims))])
    return factor_of


def normal_values(own_key, dims, deviation, reach, shards=(), held_as=jnp.bfloat16):
    values = jax.random.normal(own_key, dims, jnp.float32) * deviation
    if len(shards) > 0:
        values = levels(own_key, dims, shards, -0.22, 0.18) * values
    return jnp.clip(values, min=-reach, max=reach).astype(held_as)


def setup_inputs(seed: int = 0) -> dict:
    key_of = jax.random.split(jax.random.key(seed), 5)
    queries = draw_queries(jax.random.fold_in(key_of[4], 71), 0)
    encoded = normal_values(key_of[1], (NBR, R, D_ENC), 1.0, 6.0, ((0, 64),))
    w_kv = normal_values(key_of[2], (D_ENC, 2, D), D_ENC ** -0.5, 0.1875, ((2, 4),))
    retrieved = draw_retrieved(jax.random.fold_in(key_of[4], 71), 0)
    return {"queries": queries, "encoded": encoded, "w_kv": w_kv, "retrieved": retrieved}


def reference(queries, encoded, w_kv, retrieved):
    blocks = GROUPS // CH_DEV
    weights = w_kv.reshape(D_ENC, 2 * D).astype(jnp.float32)

    def one_block(operands):
        query_rows, tile_ids = operands
        tiles = jnp.take(encoded, tile_ids.reshape(2 * CH_DEV).astype(jnp.int32), axis=0)
        flat = jnp.dot(tiles.reshape(2 * CH_DEV * R, D_ENC).astype(jnp.float32), weights, preferred_element_type=jnp.float32)
        paired = flat.astype(jnp.bfloat16).reshape(CH_DEV, 2 * R, 2, HEADS, HEAD_DIM).astype(jnp.float32)
        key_rows = paired[:, :, 0]
        value_rows = paired[:, :, 1]
        query_heads = query_rows.reshape(CH_DEV, GROUP, HEADS, HEAD_DIM).astype(jnp.float32)
        scores = jnp.einsum("cthe,cshe->chts", query_heads, key_rows) * (HEAD_DIM ** -0.5)
        top = jnp.max(scores, axis=-1, keepdims=True)
        expd = jnp.exp(scores - top)
        probs = (expd / jnp.sum(expd, axis=-1, keepdims=True)).astype(jnp.bfloat16)
        mixed = jnp.einsum("chts,cshe->cthe", probs.astype(jnp.float32), value_rows)
        return mixed.astype(jnp.bfloat16).reshape(CH_DEV * GROUP, D)

    outputs = lax.map(one_block, (queries.reshape(blocks, CH_DEV * GROUP, D), retrieved.reshape(blocks, CH_DEV, 2)))
    return outputs.reshape(TOKENS, D)
```

```python
import functools

import jax
import jax.numpy as jnp
from jax import lax
from jax.experimental import pallas as pl
from jax.experimental.pallas import tpu as pltpu
from jax.sharding import PartitionSpec as P

GROUP = 64
HEAD_DIM = 128
TILES = 4
CORES = 2
MESH = pl.DeviceIdType.MESH
SCALE = (HEAD_DIM ** -0.5) * 1.4426950408889634


def step_distance(step, nz):
    return jnp.where(step % 2 == 1, (step + 1) // 2, (nz - step // 2) % nz)


def gather_kernel(nz, ny, ids_ref, enc_ref, w_ref, kv_ref,
                  ids_in, sel, pool, picked, rows, w_raw, w_flat, staged,
                  ids_send, ids_recv, z_send, z_recv, y_send, y_recv, x_send, x_recv, own_sem, w_sem, kv_sem):
    seq, x = lax.axis_index("seq"), lax.axis_index("mp")
    nx = lax.axis_size("mp")
    z, y, c = seq // (ny * CORES), (seq // CORES) % ny, seq % CORES
    half = x % 2
    nr = ny * CORES
    right, left = (seq, (x + 1) % nx), (seq, (x + nx - 1) % nx)

    def along_z(k):
        return (((z + k) % nz * ny + y) * CORES + c, x)

    def in_row(r):
        return ((z * ny + (y + r % ny) % ny) * CORES + (c + r // ny) % CORES, x)

    def in_row_back(r):
        return ((z * ny + (y + ny - r % ny) % ny) * CORES + (c + r // ny) % CORES, x)

    barrier = pltpu.get_barrier_semaphore()
    for k in range(1, nz):
        pl.semaphore_signal(barrier, inc=1, device_id=along_z(k), device_id_type=MESH)
    for r in range(1, nr):
        pl.semaphore_signal(barrier, inc=1, device_id=in_row(r), device_id_type=MESH)
    for to in (right, left):
        pl.semaphore_signal(barrier, inc=1, device_id=to, device_id_type=MESH)
    own_copy = pltpu.make_async_copy(enc_ref.at[:, half], pool.at[0], own_sem)
    own_copy.start()
    w_copy = pltpu.make_async_copy(w_ref, w_raw, w_sem)
    w_copy.start()
    pl.semaphore_wait(barrier, nz + nr)

    def ids_copy(r):
        return pltpu.make_async_remote_copy(ids_ref, ids_in.at[r], ids_send.at[r], ids_recv.at[r],
                                            device_id=in_row_back(r), device_id_type=MESH)

    def z_copy(step):
        k = step_distance(step, nz)
        return pltpu.make_async_remote_copy(enc_ref.at[:, half], pool.at[step], z_send.at[step], z_recv.at[step],
                                            device_id=along_z(k), device_id_type=MESH)

    def y_copy(step, r):
        return pltpu.make_async_remote_copy(picked.at[step, r], rows.at[step, r, half], y_send.at[step, r],
                                            y_recv.at[step, r], device_id=in_row(r), device_id_type=MESH)

    def x_copy(step, d):
        part = rows.at[step, pl.ds(d * ny, ny), half]
        return pltpu.make_async_remote_copy(part, part, x_send.at[step, d], x_recv.at[step, d],
                                            device_id=(right, left)[d], device_id_type=MESH)

    def x_arrival(step, d):
        part = rows.at[step, pl.ds(d * ny, ny), 1 - half]
        return pltpu.make_async_remote_copy(part, part, x_send.at[step, d], x_recv.at[step, d],
                                            device_id=(right, left)[d], device_id_type=MESH)

    for r in range(1, nr):
        ids_copy(r).start()
    for step in range(1, nz):
        z_copy(step).start()

    steps = lax.broadcasted_iota(jnp.int32, (nz, 1), 0)
    owner = ((z + nz - step_distance(steps, nz)) % nz * ny + y) * CORES + c
    for r in range(nr):
        if r > 0:
            ids_copy(r).wait_recv()
        ids = ids_ref[...] if r == 0 else ids_in[r]
        for t in range(TILES):
            hit = (ids[0:1] == owner * TILES + t) | (ids[1:2] == owner * TILES + t)
            count = jnp.sum(jnp.where(hit, 1.0, 0.0), axis=1, keepdims=True)
            sel[r, t] = jnp.broadcast_to(count, (nz, 128))

    def pick(step):
        width = pool.shape[-1] // 128
        tiles = [pool[step, t] for t in range(TILES)]
        for r in range(nr):
            total = None
            for t in range(TILES):
                lane = jnp.broadcast_to(sel[r, t, pl.ds(step, 1), :], (16, 128)).astype(jnp.bfloat16)
                term = tiles[t] * jnp.concatenate([lane] * width, axis=1)
                total = term if total is None else total + term
            if r == 0:
                rows[step, 0, half] = total
            else:
                picked[step, r] = total
                y_copy(step, r).start()

    own_copy.wait()
    pick(0)

    w_copy.wait()
    kinds = w_flat.shape[1] // 128
    per = 256 // kinds
    out_row = lax.broadcasted_iota(jnp.int32, (256, 256), 0)
    in_col = lax.broadcasted_iota(jnp.int32, (256, 256), 1)
    order = jnp.where(in_col == out_row % per * kinds + out_row // per, 1.0, 0.0).astype(jnp.bfloat16)

    def unweave(i, _):
        for u in range(2):
            b = i * 2 + u
            block = w_raw[pl.ds(pl.multiple_of(b * 256, 256), 256), :]
            sorted_rows = jnp.dot(order, block, preferred_element_type=jnp.float32).astype(jnp.bfloat16)
            for kind in range(kinds):
                at = (kind % 2) * (kinds // 2) + kind // 2
                w_flat[pl.ds(pl.multiple_of(b * per, per), per), at * 128:at * 128 + 128] = sorted_rows[kind * per:(kind + 1) * per]
        return 0

    lax.fori_loop(0, w_raw.shape[0] // 512, unweave, 0)

    def kv_copy(step):
        return pltpu.make_async_copy(staged.at[step % 2], kv_ref.at[pl.ds(step * nr, nr)], kv_sem.at[step % 2])

    def project(step):
        for d in range(2):
            x_arrival(step, d).wait_recv()

        @pl.when(step >= 2)
        def _():
            kv_copy(step - 2).wait()

        flat = rows[step].reshape(nr * 32, rows.shape[-1])

        def columns(i, _):
            at = pl.ds(pl.multiple_of(i * 512, 512), 512)
            part = jnp.dot(flat, w_flat[:, at], preferred_element_type=jnp.float32).astype(jnp.bfloat16)
            staged[step % 2, :, :, at] = part.reshape(nr, 32, 512)
            return 0

        lax.fori_loop(0, w_flat.shape[1] // 512, columns, 0)
        kv_copy(step).start()

    def body(i, _):
        @pl.when(i < nz)
        def _():
            z_copy(i).wait_recv()
            pick(i)

        @pl.when(i <= nz)
        def _():
            for d in range(2):
                for r in range(d * ny, (d + 1) * ny):
                    if r > 0:
                        y_copy(i - 1, r).wait_recv()
                x_copy(i - 1, d).start()

        @pl.when(i >= 2)
        def _():
            project(i - 2)

        return 0

    lax.fori_loop(1, nz + 2, body, 0)

    for step in range(nz - 2, nz):
        kv_copy(step).wait()
    for r in range(1, nr):
        ids_copy(r).wait_send()

    def drain(step, _):
        @pl.when(step > 0)
        def _():
            z_copy(step).wait_send()

        for r in range(1, nr):
            y_copy(step, r).wait_send()
        for d in range(2):
            x_copy(step, d).wait_send()
        return 0

    lax.fori_loop(0, nz, drain, 0)


def gather_and_project(ids, encoded, weights, nz, ny):
    count, rows, width = encoded.shape
    nr = ny * CORES
    features = weights.shape[0] * 128 // width
    dma = pltpu.SemaphoreType.DMA
    hbm = pl.BlockSpec(memory_space=pltpu.HBM)
    bf16 = jnp.bfloat16
    slots = nz * nr
    return pl.pallas_call(
        functools.partial(gather_kernel, nz, ny),
        out_shape=jax.ShapeDtypeStruct((slots, rows, features), bf16),
        in_specs=[pl.BlockSpec(memory_space=pltpu.VMEM), hbm, hbm],
        out_specs=hbm,
        scratch_shapes=[
            pltpu.VMEM((nr,) + ids.shape, jnp.int32),
            pltpu.VMEM((nr, TILES, nz, 128), jnp.float32),
            pltpu.VMEM((nz, TILES, 16, width), bf16),
            pltpu.VMEM((nz, nr, 16, width), bf16),
            pltpu.VMEM((nz, nr, 2, 16, width), bf16),
            pltpu.VMEM(weights.shape, bf16),
            pltpu.VMEM((width, features), bf16),
            pltpu.VMEM((2, nr, rows, features), bf16),
            dma((nr,)), dma((nr,)), dma((nz,)), dma((nz,)), dma((nz, nr)), dma((nz, nr)), dma((nz, 2)), dma((nz, 2)),
            dma, dma, dma((2,)),
        ],
        compiler_params=pltpu.CompilerParams(collective_id=0, has_side_effects=True, vmem_limit_bytes=58 << 20),
        cost_estimate=pl.CostEstimate(flops=2 * slots * rows * width * features, bytes_accessed=16 << 20, transcendentals=0),
    )(ids, encoded.reshape(count, 2, rows // 2, width), weights)


def attend_kernel(chunk, slots_ref, q_hbm, kv_hbm, o_hbm, q, kv, o, q_sem, kv_sem, o_sem):
    groups = q.shape[0] // GROUP
    chunks = groups // chunk
    width = q.shape[1]
    span = chunk * GROUP

    def q_copy(i):
        at = pl.ds(i * span, span)
        return pltpu.make_async_copy(q_hbm.at[at], q.at[at], q_sem.at[i])

    def o_copy(i):
        at = pl.ds(i * span, span)
        return pltpu.make_async_copy(o.at[at], o_hbm.at[at], o_sem.at[i])

    for i in range(chunks):
        q_copy(i).start()
        for j in range(2 * chunk * i, 2 * chunk * (i + 1)):
            pltpu.make_async_copy(kv_hbm.at[slots_ref[j]], kv.at[j], kv_sem.at[i]).start()

    zero = jnp.zeros((GROUP, HEAD_DIM), jnp.bfloat16)

    def step(i, _):
        q_copy(i).wait()
        part = kv.at[pl.ds(i * 2 * chunk, 2 * chunk)]
        pltpu.make_async_copy(part, part, kv_sem.at[i]).wait()
        for u in range(chunk):
            g = i * chunk + u
            row = pl.ds(pl.multiple_of(g * GROUP, GROUP), GROUP)
            both = pl.ds(2 * g, 2)
            for h in range(width // 256):
                at = slice(h * 256, h * 256 + 256)
                keys = kv[both, :, at].reshape(GROUP, 256)
                values = kv[both, :, width + h * 256:width + h * 256 + 256].reshape(GROUP, 256)
                qh = q[row, at]
                q2 = jnp.concatenate([jnp.concatenate([qh[:, :128], zero], 1), jnp.concatenate([zero, qh[:, 128:]], 1)], 0)
                scores = lax.dot_general(keys, q2, (((1,), (1,)), ((), ())), preferred_element_type=jnp.float32)
                top = jnp.max(scores, axis=0, keepdims=True)
                expd = jnp.exp2((scores - top) * SCALE)
                probs = (expd * (1.0 / jnp.sum(expd, axis=0, keepdims=True))).astype(jnp.bfloat16)
                mixed = lax.dot_general(probs, values, (((0,), (0,)), ((), ())), preferred_element_type=jnp.float32)
                o[row, at] = jnp.concatenate([mixed[:GROUP, :128], mixed[GROUP:, 128:]], 1).astype(jnp.bfloat16)
        o_copy(i).start()
        return 0

    lax.fori_loop(0, chunks, step, 0)
    for i in range(chunks):
        o_copy(i).wait()


def attend(slots, queries, kv, chunk=8):
    chunks = queries.shape[0] // GROUP // chunk
    hbm = pl.BlockSpec(memory_space=pltpu.HBM)
    dma = pltpu.SemaphoreType.DMA
    return pl.pallas_call(
        functools.partial(attend_kernel, chunk),
        out_shape=jax.ShapeDtypeStruct(queries.shape, queries.dtype),
        in_specs=[pl.BlockSpec(memory_space=pltpu.SMEM), hbm, hbm],
        out_specs=hbm,
        scratch_shapes=[pltpu.VMEM(queries.shape, jnp.bfloat16), pltpu.VMEM(kv.shape, jnp.bfloat16),
                        pltpu.VMEM(queries.shape, jnp.bfloat16), dma((chunks,)), dma((chunks,)), dma((chunks,))],
        compiler_params=pltpu.CompilerParams(vmem_limit_bytes=58 << 20),
        cost_estimate=pl.CostEstimate(flops=4 * queries.size * GROUP, bytes_accessed=17 << 20, transcendentals=queries.size // 2),
    )(slots, queries, kv)


def body(ny, queries, encoded, w_kv, retrieved):
    nz = lax.axis_size("seq") // (ny * CORES)
    seq = lax.axis_index("seq")
    z, y, c = seq // (ny * CORES), (seq // CORES) % ny, seq % CORES
    inner, _, width = w_kv.shape
    weights = w_kv.reshape(inner, 2, width // 128, 128).transpose(0, 2, 1, 3).reshape(-1, 128)
    owner = retrieved.reshape(-1) // TILES
    k = (z - owner // (ny * CORES)) % nz
    step = jnp.where(k == 0, 0, jnp.where(k <= nz // 2, 2 * k - 1, 2 * (nz - k)))
    slots = (step * CORES + (c - owner) % CORES) * ny + (y - owner // CORES) % ny
    kv = gather_and_project(retrieved.T, encoded, weights, nz, ny)
    return attend(slots.astype(jnp.int32), queries, kv)


def solution(mesh):
    in_specs = (P("seq", "mp"), P("seq", None, None), P(None, None, "mp"), P("seq", None))
    return jax.shard_map(functools.partial(body, 4), mesh=mesh, in_specs=in_specs, out_specs=P("seq", "mp"), check_vma=False)
```

```python
import functools

import jax
import jax.numpy as jnp
from jax import lax
from jax.experimental import pallas as pl
from jax.experimental.pallas import tpu as pltpu
from jax.sharding import PartitionSpec as P

GROUP = 64
HEAD_DIM = 128
TILES = 4
CORES = 2
MESH = pl.DeviceIdType.MESH
X_LAG, P_LAG = 2, 4
SCALE = (HEAD_DIM ** -0.5) * 1.4426950408889634


def step_distance(step, nz):
    return jnp.where(step % 2 == 1, (step + 1) // 2, (nz - step // 2) % nz)


def gather_kernel(nz, ny, ids_ref, enc_ref, w_ref, kv_ref,
                  ids_in, sel, pool, picked, rows, w_raw, w_flat, staged,
                  ids_send, ids_recv, z_send, z_recv, y_send, y_recv, x_send, x_recv, own_sem, w_sem, kv_sem):
    seq, x = lax.axis_index("seq"), lax.axis_index("mp")
    nx = lax.axis_size("mp")
    z, y, c = seq // (ny * CORES), (seq // CORES) % ny, seq % CORES
    half = x % 2
    nr = ny * CORES
    right, left = (seq, (x + 1) % nx), (seq, (x + nx - 1) % nx)

    def along_z(k):
        return (((z + k) % nz * ny + y) * CORES + c, x)

    def in_row(r):
        return ((z * ny + (y + r % ny) % ny) * CORES + (c + r // ny) % CORES, x)

    def in_row_back(r):
        return ((z * ny + (y + ny - r % ny) % ny) * CORES + (c + r // ny) % CORES, x)

    barrier = pltpu.get_barrier_semaphore()
    for k in range(1, nz):
        pl.semaphore_signal(barrier, inc=1, device_id=along_z(k), device_id_type=MESH)
    for r in range(1, nr):
        pl.semaphore_signal(barrier, inc=1, device_id=in_row(r), device_id_type=MESH)
    for to in (right, left):
        pl.semaphore_signal(barrier, inc=1, device_id=to, device_id_type=MESH)
    own_copy = pltpu.make_async_copy(enc_ref.at[:, half], pool.at[0], own_sem)
    own_copy.start()
    w_copy = pltpu.make_async_copy(w_ref, w_raw, w_sem)
    w_copy.start()
    pl.semaphore_wait(barrier, nz + nr)

    def ids_copy(r):
        return pltpu.make_async_remote_copy(ids_ref, ids_in.at[r], ids_send.at[r], ids_recv.at[r],
                                            device_id=in_row_back(r), device_id_type=MESH)

    def z_copy(step):
        k = step_distance(step, nz)
        return pltpu.make_async_remote_copy(enc_ref.at[:, half], pool.at[step], z_send.at[step], z_recv.at[step],
                                            device_id=along_z(k), device_id_type=MESH)

    def y_copy(step, r):
        return pltpu.make_async_remote_copy(picked.at[step, r], rows.at[step, r, half], y_send.at[step, r],
                                            y_recv.at[step, r], device_id=in_row(r), device_id_type=MESH)

    def x_copy(step, d):
        part = rows.at[step, pl.ds(d * ny, ny), half]
        return pltpu.make_async_remote_copy(part, part, x_send.at[step, d], x_recv.at[step, d],
                                            device_id=(right, left)[d], device_id_type=MESH)

    def x_arrival(step, d):
        part = rows.at[step, pl.ds(d * ny, ny), 1 - half]
        return pltpu.make_async_remote_copy(part, part, x_send.at[step, d], x_recv.at[step, d],
                                            device_id=(right, left)[d], device_id_type=MESH)

    for r in range(1, nr):
        ids_copy(r).start()
    for step in range(1, nz):
        z_copy(step).start()

    w_copy.wait()
    kinds = w_flat.shape[1] // 128
    per = 256 // kinds
    out_row = lax.broadcasted_iota(jnp.int32, (256, 256), 0)
    in_col = lax.broadcasted_iota(jnp.int32, (256, 256), 1)
    order = jnp.where(in_col == out_row % per * kinds + out_row // per, 1.0, 0.0).astype(jnp.bfloat16)

    def unweave(i, _):
        for u in range(8):
            b = i * 8 + u
            block = w_raw[pl.ds(pl.multiple_of(b * 256, 256), 256), :]
            sorted_rows = jnp.dot(order, block, preferred_element_type=jnp.float32).astype(jnp.bfloat16)
            for kind in range(kinds):
                at = (kind % 2) * (kinds // 2) + kind // 2
                w_flat[pl.ds(pl.multiple_of(b * per, per), per), at * 128:at * 128 + 128] = sorted_rows[kind * per:(kind + 1) * per]
        return 0

    lax.fori_loop(0, w_raw.shape[0] // 2048, unweave, 0)

    steps = lax.broadcasted_iota(jnp.int32, (nz, 1), 0)
    owner = ((z + nz - step_distance(steps, nz)) % nz * ny + y) * CORES + c
    for r in range(nr):
        if r > 0:
            ids_copy(r).wait_recv()
        ids = ids_ref[...] if r == 0 else ids_in[r]
        for t in range(TILES):
            hit = (ids[0:1] == owner * TILES + t) | (ids[1:2] == owner * TILES + t)
            count = jnp.sum(jnp.where(hit, 1.0, 0.0), axis=1, keepdims=True)
            sel[r, t] = jnp.broadcast_to(count, (nz, 128))

    def pick(step):
        width = pool.shape[-1] // 128
        tiles = [pool[step, t] for t in range(TILES)]
        for r in range(nr):
            total = None
            for t in range(TILES):
                lane = jnp.broadcast_to(sel[r, t, pl.ds(step, 1), :], (16, 128)).astype(jnp.bfloat16)
                term = tiles[t] * jnp.concatenate([lane] * width, axis=1)
                total = term if total is None else total + term
            if r == 0:
                rows[step, 0, half] = total
            else:
                picked[step, r] = total
                y_copy(step, r).start()

    own_copy.wait()
    pick(0)

    def kv_copy(step):
        return pltpu.make_async_copy(staged.at[step % 2], kv_ref.at[pl.ds(step * nr, nr)], kv_sem.at[step % 2])

    def project(step):
        for d in range(2):
            x_arrival(step, d).wait_recv()

        @pl.when(step >= 2)
        def _():
            kv_copy(step - 2).wait()

        flat = rows[step].reshape(nr * 32, rows.shape[-1])

        def columns(i, _):
            at = pl.ds(pl.multiple_of(i * 512, 512), 512)
            part = jnp.dot(flat, w_flat[:, at], preferred_element_type=jnp.float32).astype(jnp.bfloat16)
            staged[step % 2, :, :, at] = part.reshape(nr, 32, 512)
            return 0

        lax.fori_loop(0, w_flat.shape[1] // 512, columns, 0)
        kv_copy(step).start()

    def body(i, _):
        @pl.when(i < nz)
        def _():
            z_copy(i).wait_recv()
            pick(i)

        @pl.when((i >= X_LAG) & (i < nz + X_LAG))
        def _():
            for d in range(2):
                for r in range(d * ny, (d + 1) * ny):
                    if r > 0:
                        y_copy(i - X_LAG, r).wait_recv()
                x_copy(i - X_LAG, d).start()

        @pl.when(i >= P_LAG)
        def _():
            project(i - P_LAG)

        return 0

    lax.fori_loop(1, nz + P_LAG, body, 0)

    for step in range(nz - 2, nz):
        kv_copy(step).wait()
    for r in range(1, nr):
        ids_copy(r).wait_send()

    def drain(step, _):
        @pl.when(step > 0)
        def _():
            z_copy(step).wait_send()

        for r in range(1, nr):
            y_copy(step, r).wait_send()
        for d in range(2):
            x_copy(step, d).wait_send()
        return 0

    lax.fori_loop(0, nz, drain, 0)


def gather_and_project(ids, encoded, weights, nz, ny):
    count, rows, width = encoded.shape
    nr = ny * CORES
    features = weights.shape[0] * 128 // width
    dma = pltpu.SemaphoreType.DMA
    hbm = pl.BlockSpec(memory_space=pltpu.HBM)
    bf16 = jnp.bfloat16
    slots = nz * nr
    return pl.pallas_call(
        functools.partial(gather_kernel, nz, ny),
        out_shape=jax.ShapeDtypeStruct((slots, rows, features), bf16),
        in_specs=[pl.BlockSpec(memory_space=pltpu.VMEM), hbm, hbm],
        out_specs=hbm,
        scratch_shapes=[
            pltpu.VMEM((nr,) + ids.shape, jnp.int32),
            pltpu.VMEM((nr, TILES, nz, 128), jnp.float32),
            pltpu.VMEM((nz, TILES, 16, width), bf16),
            pltpu.VMEM((nz, nr, 16, width), bf16),
            pltpu.VMEM((nz, nr, 2, 16, width), bf16),
            pltpu.VMEM(weights.shape, bf16),
            pltpu.VMEM((width, features), bf16),
            pltpu.VMEM((2, nr, rows, features), bf16),
            dma((nr,)), dma((nr,)), dma((nz,)), dma((nz,)), dma((nz, nr)), dma((nz, nr)), dma((nz, 2)), dma((nz, 2)),
            dma, dma, dma((2,)),
        ],
        compiler_params=pltpu.CompilerParams(collective_id=0, has_side_effects=True, vmem_limit_bytes=58 << 20),
        cost_estimate=pl.CostEstimate(flops=2 * slots * rows * width * features, bytes_accessed=16 << 20, transcendentals=0),
    )(ids, encoded.reshape(count, 2, rows // 2, width), weights)


def attend_kernel(chunk, nz, ny, ids_ref, q_hbm, kv_hbm, o_hbm, q, kv, o, q_sem, kv_sem, o_sem):
    groups = q.shape[0] // GROUP
    chunks = groups // chunk
    width = q.shape[1]
    span = chunk * GROUP

    def q_copy(i):
        at = pl.ds(i * span, span)
        return pltpu.make_async_copy(q_hbm.at[at], q.at[at], q_sem.at[i])

    def o_copy(i):
        at = pl.ds(i * span, span)
        return pltpu.make_async_copy(o.at[at], o_hbm.at[at], o_sem.at[i])

    seq = lax.axis_index("seq")
    z, y, c = seq // (ny * CORES), (seq // CORES) % ny, seq % CORES

    def slot_of(tile):
        owner = tile // TILES
        k = (z + nz - owner // (ny * CORES)) % nz
        step = jnp.where(k == 0, 0, jnp.where(k <= nz // 2, 2 * k - 1, 2 * (nz - k)))
        return (step * CORES + (c + owner) % CORES) * ny + (y + ny - owner // CORES % ny) % ny

    for i in range(chunks):
        q_copy(i).start()
        for j in range(2 * chunk * i, 2 * chunk * (i + 1)):
            pltpu.make_async_copy(kv_hbm.at[slot_of(ids_ref[j % 2, j // 2])], kv.at[j], kv_sem.at[i]).start()

    zero = jnp.zeros((GROUP, HEAD_DIM), jnp.bfloat16)

    def step(i, _):
        q_copy(i).wait()
        part = kv.at[pl.ds(i * 2 * chunk, 2 * chunk)]
        pltpu.make_async_copy(part, part, kv_sem.at[i]).wait()
        rows = [pl.ds(pl.multiple_of((i * chunk + u) * GROUP, GROUP), GROUP) for u in range(chunk)]
        units = [(u, h * 256) for u in range(chunk) for h in range(width // 256)]

        def tile_rows(u, at):
            return kv[pl.ds(2 * (i * chunk + u), 2), :, at:at + 256].reshape(GROUP, 256)

        all_scores = []
        for u, at in units:
            qh = q[rows[u], at:at + 256]
            q2 = jnp.concatenate([jnp.concatenate([qh[:, :128], zero], 1), jnp.concatenate([zero, qh[:, 128:]], 1)], 0)
            all_scores.append(lax.dot_general(tile_rows(u, at), q2, (((1,), (1,)), ((), ())), preferred_element_type=jnp.float32))
        all_probs = []
        for scores in all_scores:
            top = jnp.max(scores, axis=0, keepdims=True)
            expd = jnp.exp2((scores - top) * SCALE)
            all_probs.append((expd * (1.0 / jnp.sum(expd, axis=0, keepdims=True))).astype(jnp.bfloat16))
        for (u, at), probs in zip(units, all_probs):
            mixed = lax.dot_general(probs, tile_rows(u, width + at), (((0,), (0,)), ((), ())), preferred_element_type=jnp.float32)
            o[rows[u], at:at + 256] = jnp.concatenate([mixed[:GROUP, :128], mixed[GROUP:, 128:]], 1).astype(jnp.bfloat16)
        o_copy(i).start()
        return 0

    lax.fori_loop(0, chunks, step, 0)
    for i in range(chunks):
        o_copy(i).wait()


def attend(ids, queries, kv, nz, ny, chunk=4):
    chunks = queries.shape[0] // GROUP // chunk
    hbm = pl.BlockSpec(memory_space=pltpu.HBM)
    dma = pltpu.SemaphoreType.DMA
    return pl.pallas_call(
        functools.partial(attend_kernel, chunk, nz, ny),
        out_shape=jax.ShapeDtypeStruct(queries.shape, queries.dtype),
        in_specs=[pl.BlockSpec(memory_space=pltpu.SMEM), hbm, hbm],
        out_specs=hbm,
        scratch_shapes=[pltpu.VMEM(queries.shape, jnp.bfloat16), pltpu.VMEM(kv.shape, jnp.bfloat16),
                        pltpu.VMEM(queries.shape, jnp.bfloat16), dma((chunks,)), dma((chunks,)), dma((chunks,))],
        compiler_params=pltpu.CompilerParams(vmem_limit_bytes=58 << 20),
        cost_estimate=pl.CostEstimate(flops=4 * queries.size * GROUP, bytes_accessed=17 << 20, transcendentals=queries.size // 2),
    )(ids, queries, kv)


def body(ny, queries, encoded, w_kv, retrieved):
    nz = lax.axis_size("seq") // (ny * CORES)
    inner, _, width = w_kv.shape
    weights = w_kv.reshape(inner, 2, width // 128, 128).transpose(0, 2, 1, 3).reshape(-1, 128)
    ids = retrieved.T
    kv = gather_and_project(ids, encoded, weights, nz, ny)
    return attend(ids, queries, kv, nz, ny)


def solution(mesh):
    in_specs = (P("seq", "mp"), P("seq", None, None), P(None, None, "mp"), P("seq", None))
    return jax.shard_map(functools.partial(body, 4), mesh=mesh, in_specs=in_specs, out_specs=P("seq", "mp"), check_vma=False)
```

```python
import functools

import jax
import jax.numpy as jnp
from jax import lax
from jax.experimental import pallas as pl
from jax.experimental.pallas import tpu as pltpu
from jax.sharding import PartitionSpec as P

GROUP = 64
HEAD_DIM = 128
TILES = 4
CORES = 2
MESH = pl.DeviceIdType.MESH
X_LAG, P_LAG = 2, 4
SCALE = (HEAD_DIM ** -0.5) * 1.4426950408889634


def step_distance(step, nz):
    return jnp.where(step % 2 == 1, (step + 1) // 2, (nz - step // 2) % nz)


def gather_kernel(nz, ny, ids_ref, enc_ref, w_ref, kv_ref,
                  ids_in, sel, pool, picked, rows, w_raw, w_flat,
                  ids_send, ids_recv, z_send, z_recv, y_send, y_recv, x_send, x_recv, own_sem, w_sem):
    seq, x = lax.axis_index("seq"), lax.axis_index("mp")
    nx = lax.axis_size("mp")
    z, y, c = seq // (ny * CORES), (seq // CORES) % ny, seq % CORES
    half = x % 2
    nr = ny * CORES
    right, left = (seq, (x + 1) % nx), (seq, (x + nx - 1) % nx)

    def along_z(k):
        return (((z + k) % nz * ny + y) * CORES + c, x)

    def in_row(r):
        return ((z * ny + (y + r % ny) % ny) * CORES + (c + r // ny) % CORES, x)

    def in_row_back(r):
        return ((z * ny + (y + ny - r % ny) % ny) * CORES + (c + r // ny) % CORES, x)

    barrier = pltpu.get_barrier_semaphore()
    for k in range(1, nz):
        pl.semaphore_signal(barrier, inc=1, device_id=along_z(k), device_id_type=MESH)
    for r in range(1, nr):
        pl.semaphore_signal(barrier, inc=1, device_id=in_row(r), device_id_type=MESH)
    for to in (right, left):
        pl.semaphore_signal(barrier, inc=1, device_id=to, device_id_type=MESH)
    own_copy = pltpu.make_async_copy(enc_ref.at[:, half], pool.at[0], own_sem)
    own_copy.start()
    w_copy = pltpu.make_async_copy(w_ref, w_raw, w_sem)
    w_copy.start()
    pl.semaphore_wait(barrier, nz + nr)

    def ids_copy(r):
        return pltpu.make_async_remote_copy(ids_ref, ids_in.at[r], ids_send.at[r], ids_recv.at[r],
                                            device_id=in_row_back(r), device_id_type=MESH)

    def z_copy(step):
        k = step_distance(step, nz)
        return pltpu.make_async_remote_copy(enc_ref.at[:, half], pool.at[step], z_send.at[step], z_recv.at[step],
                                            device_id=along_z(k), device_id_type=MESH)

    def y_copy(step, r):
        return pltpu.make_async_remote_copy(picked.at[step, r], rows.at[step, r, half], y_send.at[step, r],
                                            y_recv.at[step, r], device_id=in_row(r), device_id_type=MESH)

    def x_copy(step, d):
        part = rows.at[step, pl.ds(d * ny, ny), half]
        return pltpu.make_async_remote_copy(part, part, x_send.at[step, d], x_recv.at[step, d],
                                            device_id=(right, left)[d], device_id_type=MESH)

    def x_arrival(step, d):
        part = rows.at[step, pl.ds(d * ny, ny), 1 - half]
        return pltpu.make_async_remote_copy(part, part, x_send.at[step, d], x_recv.at[step, d],
                                            device_id=(right, left)[d], device_id_type=MESH)

    for r in range(1, nr):
        ids_copy(r).start()
    for step in range(1, nz):
        z_copy(step).start()

    w_copy.wait()
    kinds = w_flat.shape[1] // 128
    per = 256 // kinds
    out_row = lax.broadcasted_iota(jnp.int32, (256, 256), 0)
    in_col = lax.broadcasted_iota(jnp.int32, (256, 256), 1)
    order = jnp.where(in_col == out_row % per * kinds + out_row // per, 1.0, 0.0).astype(jnp.bfloat16)

    def unweave(i, _):
        for u in range(8):
            b = i * 8 + u
            block = w_raw[pl.ds(pl.multiple_of(b * 256, 256), 256), :]
            sorted_rows = jnp.dot(order, block, preferred_element_type=jnp.float32).astype(jnp.bfloat16)
            for kind in range(kinds):
                at = (kind % 2) * (kinds // 2) + kind // 2
                w_flat[pl.ds(pl.multiple_of(b * per, per), per), at * 128:at * 128 + 128] = sorted_rows[kind * per:(kind + 1) * per]
        return 0

    lax.fori_loop(0, w_raw.shape[0] // 2048, unweave, 0)

    steps = lax.broadcasted_iota(jnp.int32, (nz, 1), 0)
    owner = ((z + nz - step_distance(steps, nz)) % nz * ny + y) * CORES + c
    for r in range(nr):
        if r > 0:
            ids_copy(r).wait_recv()
        ids = ids_ref[...] if r == 0 else ids_in[r]
        for t in range(TILES):
            hit = (ids[0:1] == owner * TILES + t) | (ids[1:2] == owner * TILES + t)
            count = jnp.sum(jnp.where(hit, 1.0, 0.0), axis=1, keepdims=True)
            sel[r, t] = jnp.broadcast_to(count, (nz, 128))

    def pick(step):
        width = pool.shape[-1] // 128
        tiles = [pool[step, t] for t in range(TILES)]
        for r in range(nr):
            total = None
            for t in range(TILES):
                lane = jnp.broadcast_to(sel[r, t, pl.ds(step, 1), :], (16, 128)).astype(jnp.bfloat16)
                term = tiles[t] * jnp.concatenate([lane] * width, axis=1)
                total = term if total is None else total + term
            if r == 0:
                rows[step, 0, half] = total
            else:
                picked[step, r] = total
                y_copy(step, r).start()

    own_copy.wait()
    pick(0)

    def project(step):
        for d in range(2):
            x_arrival(step, d).wait_recv()

        flat = rows[step].reshape(nr * 32, rows.shape[-1])

        def columns(i, _):
            at = pl.ds(pl.multiple_of(i * 512, 512), 512)
            part = jnp.dot(flat, w_flat[:, at], preferred_element_type=jnp.float32).astype(jnp.bfloat16)
            kv_ref[pl.ds(step * nr, nr), :, at] = part.reshape(nr, 32, 512)
            return 0

        lax.fori_loop(0, w_flat.shape[1] // 512, columns, 0)

    def body(i, _):
        @pl.when(i < nz)
        def _():
            z_copy(i).wait_recv()
            pick(i)

        @pl.when((i >= X_LAG) & (i < nz + X_LAG))
        def _():
            for d in range(2):
                for r in range(d * ny, (d + 1) * ny):
                    if r > 0:
                        y_copy(i - X_LAG, r).wait_recv()
                x_copy(i - X_LAG, d).start()

        @pl.when(i >= P_LAG)
        def _():
            project(i - P_LAG)

        return 0

    lax.fori_loop(1, nz + P_LAG, body, 0)

    for r in range(1, nr):
        ids_copy(r).wait_send()

    def drain(step, _):
        @pl.when(step > 0)
        def _():
            z_copy(step).wait_send()

        for r in range(1, nr):
            y_copy(step, r).wait_send()
        for d in range(2):
            x_copy(step, d).wait_send()
        return 0

    lax.fori_loop(0, nz, drain, 0)


def gather_and_project(ids, encoded, weights, nz, ny):
    rows, width = 2 * encoded.shape[2], encoded.shape[3]
    nr = ny * CORES
    features = weights.shape[0] * 128 // width
    dma = pltpu.SemaphoreType.DMA
    hbm = pl.BlockSpec(memory_space=pltpu.HBM)
    bf16 = jnp.bfloat16
    slots = nz * nr
    return pl.pallas_call(
        functools.partial(gather_kernel, nz, ny),
        out_shape=jax.ShapeDtypeStruct((slots, rows, features), bf16),
        in_specs=[pl.BlockSpec(memory_space=pltpu.VMEM), hbm, hbm],
        out_specs=pl.BlockSpec(memory_space=pltpu.VMEM),
        scratch_shapes=[
            pltpu.VMEM((nr,) + ids.shape, jnp.int32),
            pltpu.VMEM((nr, TILES, nz, 128), jnp.float32),
            pltpu.VMEM((nz, TILES, 16, width), bf16),
            pltpu.VMEM((nz, nr, 16, width), bf16),
            pltpu.VMEM((nz, nr, 2, 16, width), bf16),
            pltpu.VMEM(weights.shape, bf16),
            pltpu.VMEM((width, features), bf16),
            dma((nr,)), dma((nr,)), dma((nz,)), dma((nz,)), dma((nz, nr)), dma((nz, nr)), dma((nz, 2)), dma((nz, 2)),
            dma, dma,
        ],
        compiler_params=pltpu.CompilerParams(collective_id=0, has_side_effects=True, vmem_limit_bytes=20 << 20),
        cost_estimate=pl.CostEstimate(flops=2 * slots * rows * width * features, bytes_accessed=16 << 20, transcendentals=0),
    )(ids, encoded, weights)


def attend_kernel(chunk, nz, ny, ids_ref, q, kv, o_hbm, o, o_sem):
    groups = q.shape[0] // GROUP
    chunks = groups // chunk
    width = q.shape[1]
    span = chunk * GROUP

    def o_copy(i):
        at = pl.ds(i * span, span)
        return pltpu.make_async_copy(o.at[at], o_hbm.at[at], o_sem.at[i])

    seq = lax.axis_index("seq")
    z, y, c = seq // (ny * CORES), (seq // CORES) % ny, seq % CORES

    def slot_of(tile):
        owner = tile // TILES
        k = (z + nz - owner // (ny * CORES)) % nz
        step = jnp.where(k == 0, 0, jnp.where(k <= nz // 2, 2 * k - 1, 2 * (nz - k)))
        return (step * CORES + (c + owner) % CORES) * ny + (y + ny - owner // CORES % ny) % ny

    zero = jnp.zeros((GROUP, HEAD_DIM), jnp.bfloat16)

    def step(i, _):
        slots = [[slot_of(ids_ref[j, i * chunk + u]) for j in range(2)] for u in range(chunk)]
        rows = [pl.ds(pl.multiple_of((i * chunk + u) * GROUP, GROUP), GROUP) for u in range(chunk)]
        units = [(u, h * 256) for u in range(chunk) for h in range(width // 256)]

        def tile_rows(u, at):
            return jnp.concatenate([kv[slot, :, at:at + 256] for slot in slots[u]], 0)

        all_scores = []
        for u, at in units:
            qh = q[rows[u], at:at + 256]
            q2 = jnp.concatenate([jnp.concatenate([qh[:, :128], zero], 1), jnp.concatenate([zero, qh[:, 128:]], 1)], 0)
            all_scores.append(lax.dot_general(tile_rows(u, at), q2, (((1,), (1,)), ((), ())), preferred_element_type=jnp.float32))
        all_probs = []
        for scores in all_scores:
            top = jnp.max(scores, axis=0, keepdims=True)
            expd = jnp.exp2((scores - top) * SCALE)
            all_probs.append((expd * (1.0 / jnp.sum(expd, axis=0, keepdims=True))).astype(jnp.bfloat16))
        for (u, at), probs in zip(units, all_probs):
            mixed = lax.dot_general(probs, tile_rows(u, width + at), (((0,), (0,)), ((), ())), preferred_element_type=jnp.float32)
            o[rows[u], at:at + 256] = jnp.concatenate([mixed[:GROUP, :128], mixed[GROUP:, 128:]], 1).astype(jnp.bfloat16)
        o_copy(i).start()
        return 0

    lax.fori_loop(0, chunks, step, 0)
    for i in range(chunks):
        o_copy(i).wait()


def attend(ids, queries, kv, nz, ny, chunk=8):
    chunks = queries.shape[0] // GROUP // chunk
    vmem = pl.BlockSpec(memory_space=pltpu.VMEM)
    hbm = pl.BlockSpec(memory_space=pltpu.HBM)
    dma = pltpu.SemaphoreType.DMA
    return pl.pallas_call(
        functools.partial(attend_kernel, chunk, nz, ny),
        out_shape=jax.ShapeDtypeStruct(queries.shape, queries.dtype),
        in_specs=[pl.BlockSpec(memory_space=pltpu.SMEM), vmem, vmem],
        out_specs=hbm,
        scratch_shapes=[pltpu.VMEM(queries.shape, jnp.bfloat16), dma((chunks,))],
        compiler_params=pltpu.CompilerParams(vmem_limit_bytes=20 << 20),
        cost_estimate=pl.CostEstimate(flops=4 * queries.size * GROUP, bytes_accessed=17 << 20, transcendentals=queries.size // 2),
    )(ids, queries, kv)


def body(ny, queries, encoded, w_kv, retrieved):
    nz = lax.axis_size("seq") // (ny * CORES)
    inner, _, width = w_kv.shape
    weights = w_kv.reshape(inner, 2, width // 128, 128).transpose(0, 2, 1, 3).reshape(-1, 128)
    ids = retrieved.T
    kv = gather_and_project(ids, pltpu.with_memory_space_constraint(encoded.reshape(encoded.shape[0], 2, -1, inner), pltpu.HBM),
                            pltpu.with_memory_space_constraint(weights, pltpu.HBM), nz, ny)
    return attend(ids, queries, kv, nz, ny)


def solution(mesh):
    in_specs = (P("seq", "mp"), P("seq", None, None), P(None, None, "mp"), P("seq", None))
    return jax.shard_map(functools.partial(body, 4), mesh=mesh, in_specs=in_specs, out_specs=P("seq", "mp"), check_vma=False)
```

```python
import functools

import jax
import jax.numpy as jnp
from jax import lax
from jax.experimental import pallas as pl
from jax.experimental.pallas import tpu as pltpu
from jax.sharding import PartitionSpec as P

GROUP = 64
HEAD_DIM = 128
TILES = 4
CORES = 2
MESH = pl.DeviceIdType.MESH
X_LAG, P_LAG = 2, 4
SCALE = (HEAD_DIM ** -0.5) * 1.4426950408889634


def step_distance(step, nz):
    near = jnp.where(step % 2 == 1, (step + 1) // 2, (nz - step // 2) % nz)
    return jnp.where(step < 5, near, jnp.where(step == 5, nz // 2, jnp.where(step == 6, 3, nz - 3)))


def distance_step(k, nz):
    near = jnp.where(k == 0, 0, jnp.where(k <= 2, 2 * k - 1, 2 * (nz - k)))
    return jnp.where(k == nz // 2, 5, jnp.where(k == 3, 6, jnp.where(k == nz - 3, 7, near)))


def gather_kernel(nz, ny, ids_hbm, enc_ref, w_ref, kv_ref,
                  ids_ref, ids_in, sel, pool, picked, rows, w_raw, w_flat,
                  ids_send, ids_recv, z_send, z_recv, y_send, y_recv, x_send, x_recv, own_sem, w_sem, ids_sem):
    seq, x = lax.axis_index("seq"), lax.axis_index("mp")
    nx = lax.axis_size("mp")
    z, y, c = seq // (ny * CORES), (seq // CORES) % ny, seq % CORES
    half = x % 2
    nr = ny * CORES
    right, left = (seq, (x + 1) % nx), (seq, (x + nx - 1) % nx)

    def along_z(k):
        return (((z + k) % nz * ny + y) * CORES + c, x)

    def in_row(r):
        return ((z * ny + (y + r % ny) % ny) * CORES + (c + r // ny) % CORES, x)

    def in_row_back(r):
        return ((z * ny + (y + ny - r % ny) % ny) * CORES + (c + r // ny) % CORES, x)

    ids_load = pltpu.make_async_copy(ids_hbm, ids_ref, ids_sem)
    ids_load.start()
    barrier = pltpu.get_barrier_semaphore()
    for k in (1, nz - 1, 2, nz - 2, nz // 2):
        pl.semaphore_signal(barrier, inc=1, device_id=along_z(k), device_id_type=MESH)
    for r in range(1, nr):
        pl.semaphore_signal(barrier, inc=1, device_id=in_row(r), device_id_type=MESH)
    for to in (right, left):
        pl.semaphore_signal(barrier, inc=1, device_id=to, device_id_type=MESH)
    own_copy = pltpu.make_async_copy(enc_ref.at[:, half], pool.at[0], own_sem)
    own_copy.start()
    w_copy = pltpu.make_async_copy(w_ref, w_raw, w_sem)
    w_copy.start()
    ids_load.wait()
    pl.semaphore_wait(barrier, 5 + (nr - 1) + 2)

    def ids_copy(r):
        return pltpu.make_async_remote_copy(ids_ref, ids_in.at[r], ids_send.at[r], ids_recv.at[r],
                                            device_id=in_row_back(r), device_id_type=MESH)

    def z_copy(step):
        k = step_distance(step, nz)
        return pltpu.make_async_remote_copy(enc_ref.at[:, half], pool.at[step], z_send.at[step], z_recv.at[step],
                                            device_id=along_z(k), device_id_type=MESH)

    def pass_on(step):
        return pltpu.make_async_remote_copy(pool.at[step], pool.at[step + 3], z_send.at[step + 3], z_recv.at[step + 3],
                                            device_id=along_z(jnp.where(step == 3, 1, nz - 1)), device_id_type=MESH)

    def y_copy(step, r):
        return pltpu.make_async_remote_copy(picked.at[step, r], rows.at[step, r, half], y_send.at[step, r],
                                            y_recv.at[step, r], device_id=in_row(r), device_id_type=MESH)

    def x_copy(step, d):
        part = rows.at[step, pl.ds(d * ny, ny), half]
        return pltpu.make_async_remote_copy(part, part, x_send.at[step, d], x_recv.at[step, d],
                                            device_id=(right, left)[d], device_id_type=MESH)

    def x_arrival(step, d):
        part = rows.at[step, pl.ds(d * ny, ny), 1 - half]
        return pltpu.make_async_remote_copy(part, part, x_send.at[step, d], x_recv.at[step, d],
                                            device_id=(right, left)[d], device_id_type=MESH)

    for r in range(1, nr):
        ids_copy(r).start()
    for step in range(1, 6):
        z_copy(step).start()

    w_copy.wait()
    kinds = w_flat.shape[1] // 128
    per = 256 // kinds
    out_row = lax.broadcasted_iota(jnp.int32, (256, 256), 0)
    in_col = lax.broadcasted_iota(jnp.int32, (256, 256), 1)
    order = jnp.where(in_col == out_row % per * kinds + out_row // per, 1.0, 0.0).astype(jnp.bfloat16)

    def unweave(i, _):
        for u in range(8):
            b = i * 8 + u
            block = w_raw[pl.ds(pl.multiple_of(b * 256, 256), 256), :]
            sorted_rows = jnp.dot(order, block, preferred_element_type=jnp.float32).astype(jnp.bfloat16)
            for kind in range(kinds):
                at = (kind % 2) * (kinds // 2) + kind // 2
                w_flat[pl.ds(pl.multiple_of(b * per, per), per), at * 128:at * 128 + 128] = sorted_rows[kind * per:(kind + 1) * per]
        return 0

    lax.fori_loop(0, w_raw.shape[0] // 2048, unweave, 0)

    steps = lax.broadcasted_iota(jnp.int32, (nz, 1), 0)
    owner = ((z + nz - step_distance(steps, nz)) % nz * ny + y) * CORES + c
    for r in range(nr):
        if r > 0:
            ids_copy(r).wait_recv()
        ids = ids_ref[...] if r == 0 else ids_in[r]
        for t in range(TILES):
            hit = (ids[0:1] == owner * TILES + t) | (ids[1:2] == owner * TILES + t)
            count = jnp.sum(jnp.where(hit, 1.0, 0.0), axis=1, keepdims=True)
            sel[r, t] = jnp.broadcast_to(count, (nz, 128))

    def pick(step):
        width = pool.shape[-1] // 128
        tiles = [pool[step, t] for t in range(TILES)]
        for r in range(nr):
            total = None
            for t in range(TILES):
                lane = jnp.broadcast_to(sel[r, t, pl.ds(step, 1), :], (16, 128)).astype(jnp.bfloat16)
                term = tiles[t] * jnp.concatenate([lane] * width, axis=1)
                total = term if total is None else total + term
            if r == 0:
                rows[step, 0, half] = total
            else:
                picked[step, r] = total
                y_copy(step, r).start()

    own_copy.wait()
    pick(0)

    def project(step):
        for d in range(2):
            x_arrival(step, d).wait_recv()

        flat = rows[step].reshape(nr * 32, rows.shape[-1])

        def columns(i, _):
            at = pl.ds(pl.multiple_of(i * 512, 512), 512)
            part = jnp.dot(flat, w_flat[:, at], preferred_element_type=jnp.float32).astype(jnp.bfloat16)
            kv_ref[pl.ds(step * nr, nr), :, at] = part.reshape(nr, 32, 512)
            return 0

        lax.fori_loop(0, w_flat.shape[1] // 512, columns, 0)

    def body(i, _):
        @pl.when(i < nz)
        def _():
            z_copy(i).wait_recv()

            @pl.when((i == 3) | (i == 4))
            def _():
                pass_on(i).start()

            pick(i)

        @pl.when((i >= X_LAG) & (i < nz + X_LAG))
        def _():
            for d in range(2):
                for r in range(d * ny, (d + 1) * ny):
                    if r > 0:
                        y_copy(i - X_LAG, r).wait_recv()
                x_copy(i - X_LAG, d).start()

        @pl.when(i >= P_LAG)
        def _():
            project(i - P_LAG)

        return 0

    lax.fori_loop(1, nz + P_LAG, body, 0)

    for r in range(1, nr):
        ids_copy(r).wait_send()

    def drain(step, _):
        @pl.when(step > 0)
        def _():
            z_copy(step).wait_send()

        for r in range(1, nr):
            y_copy(step, r).wait_send()
        for d in range(2):
            x_copy(step, d).wait_send()
        return 0

    lax.fori_loop(0, nz, drain, 0)


def gather_and_project(ids, encoded, weights, nz, ny):
    rows, width = 2 * encoded.shape[2], encoded.shape[3]
    nr = ny * CORES
    features = weights.shape[0] * 128 // width
    dma = pltpu.SemaphoreType.DMA
    hbm = pl.BlockSpec(memory_space=pltpu.HBM)
    bf16 = jnp.bfloat16
    slots = nz * nr
    return pl.pallas_call(
        functools.partial(gather_kernel, nz, ny),
        out_shape=jax.ShapeDtypeStruct((slots, rows, features), bf16),
        in_specs=[hbm, hbm, hbm],
        out_specs=pl.BlockSpec(memory_space=pltpu.VMEM),
        scratch_shapes=[
            pltpu.VMEM(ids.shape, jnp.int32),
            pltpu.VMEM((nr,) + ids.shape, jnp.int32),
            pltpu.VMEM((nr, TILES, nz, 128), jnp.float32),
            pltpu.VMEM((nz, TILES, 16, width), bf16),
            pltpu.VMEM((nz, nr, 16, width), bf16),
            pltpu.VMEM((nz, nr, 2, 16, width), bf16),
            pltpu.VMEM(weights.shape, bf16),
            pltpu.VMEM((width, features), bf16),
            dma((nr,)), dma((nr,)), dma((nz,)), dma((nz,)), dma((nz, nr)), dma((nz, nr)), dma((nz, 2)), dma((nz, 2)),
            dma, dma, dma,
        ],
        compiler_params=pltpu.CompilerParams(collective_id=0, has_side_effects=True, vmem_limit_bytes=20 << 20),
        cost_estimate=pl.CostEstimate(flops=2 * slots * rows * width * features, bytes_accessed=16 << 20, transcendentals=0),
    )(ids, encoded, weights)


def attend_kernel(chunk, nz, ny, ids_ref, q, kv, o_hbm, o, o_sem):
    groups = q.shape[0] // GROUP
    chunks = groups // chunk
    width = q.shape[1]
    span = chunk * GROUP

    def o_copy(i):
        at = pl.ds(i * span, span)
        return pltpu.make_async_copy(o.at[at], o_hbm.at[at], o_sem.at[i])

    seq = lax.axis_index("seq")
    z, y, c = seq // (ny * CORES), (seq // CORES) % ny, seq % CORES

    def slot_of(tile):
        owner = tile // TILES
        k = (z + nz - owner // (ny * CORES)) % nz
        return (distance_step(k, nz) * CORES + (c + owner) % CORES) * ny + (y + ny - owner // CORES % ny) % ny

    zero = jnp.zeros((GROUP, HEAD_DIM), jnp.bfloat16)

    def step(i, _):
        slots = [[slot_of(ids_ref[j, i * chunk + u]) for j in range(2)] for u in range(chunk)]
        rows = [pl.ds(pl.multiple_of((i * chunk + u) * GROUP, GROUP), GROUP) for u in range(chunk)]
        units = [(u, h * 256) for u in range(chunk) for h in range(width // 256)]

        def tile_rows(u, at):
            return jnp.concatenate([kv[slot, :, at:at + 256] for slot in slots[u]], 0)

        all_scores = []
        for u, at in units:
            qh = q[rows[u], at:at + 256]
            q2 = jnp.concatenate([jnp.concatenate([qh[:, :128], zero], 1), jnp.concatenate([zero, qh[:, 128:]], 1)], 0)
            all_scores.append(lax.dot_general(tile_rows(u, at), q2, (((1,), (1,)), ((), ())), preferred_element_type=jnp.float32))
        all_probs = []
        for scores in all_scores:
            top = jnp.max(scores, axis=0, keepdims=True)
            expd = jnp.exp2((scores - top) * SCALE)
            all_probs.append((expd * (1.0 / jnp.sum(expd, axis=0, keepdims=True))).astype(jnp.bfloat16))
        for (u, at), probs in zip(units, all_probs):
            mixed = lax.dot_general(probs, tile_rows(u, width + at), (((0,), (0,)), ((), ())), preferred_element_type=jnp.float32)
            o[rows[u], at:at + 256] = jnp.concatenate([mixed[:GROUP, :128], mixed[GROUP:, 128:]], 1).astype(jnp.bfloat16)
        o_copy(i).start()
        return 0

    lax.fori_loop(0, chunks, step, 0)
    for i in range(chunks):
        o_copy(i).wait()


def attend(ids, queries, kv, nz, ny, chunk=8):
    chunks = queries.shape[0] // GROUP // chunk
    vmem = pl.BlockSpec(memory_space=pltpu.VMEM)
    hbm = pl.BlockSpec(memory_space=pltpu.HBM)
    dma = pltpu.SemaphoreType.DMA
    return pl.pallas_call(
        functools.partial(attend_kernel, chunk, nz, ny),
        out_shape=jax.ShapeDtypeStruct(queries.shape, queries.dtype),
        in_specs=[pl.BlockSpec(memory_space=pltpu.SMEM), vmem, vmem],
        out_specs=hbm,
        scratch_shapes=[pltpu.VMEM(queries.shape, jnp.bfloat16), dma((chunks,))],
        compiler_params=pltpu.CompilerParams(vmem_limit_bytes=20 << 20),
        cost_estimate=pl.CostEstimate(flops=4 * queries.size * GROUP, bytes_accessed=17 << 20, transcendentals=queries.size // 2),
    )(ids, queries, kv)


def body(ny, queries, encoded, w_kv, retrieved):
    nz = lax.axis_size("seq") // (ny * CORES)
    inner, _, width = w_kv.shape
    weights = w_kv.reshape(inner, 2, width // 128, 128).transpose(0, 2, 1, 3).reshape(-1, 128)
    in_hbm = functools.partial(pltpu.with_memory_space_constraint, memory_space=pltpu.HBM)
    ids = in_hbm(retrieved.T)
    kv = gather_and_project(ids, in_hbm(encoded.reshape(encoded.shape[0], 2, -1, inner)), in_hbm(weights), nz, ny)
    return attend(ids, queries, kv, nz, ny)


def solution(mesh):
    in_specs = (P("seq", "mp"), P("seq", None, None), P(None, None, "mp"), P("seq", None))
    return jax.shard_map(functools.partial(body, 4), mesh=mesh, in_specs=in_specs, out_specs=P("seq", "mp"), check_vma=False)
```

```python
import functools

import jax
import jax.numpy as jnp
from jax import lax
from jax.experimental import pallas as pl
from jax.experimental.pallas import tpu as pltpu
from jax.sharding import PartitionSpec as P

GROUP = 64
HEAD_DIM = 128
TILES = 4
CORES = 2
MESH = pl.DeviceIdType.MESH
X_LAG, P_LAG = 2, 4
SCALE = (HEAD_DIM ** -0.5) * 1.4426950408889634


def step_distance(step, nz):
    near = jnp.where(step % 2 == 1, (step + 1) // 2, (nz - step // 2) % nz)
    return jnp.where(step < 5, near, jnp.where(step == 5, nz // 2, jnp.where(step == 6, 3, nz - 3)))


def distance_step(k, nz):
    near = jnp.where(k == 0, 0, jnp.where(k <= 2, 2 * k - 1, 2 * (nz - k)))
    return jnp.where(k == nz // 2, 5, jnp.where(k == 3, 6, jnp.where(k == nz - 3, 7, near)))


def gather_kernel(nz, ny, ids_hbm, enc_ref, w_ref, kv_ref,
                  ids_ref, ids_in, sel, pool, picked, mine, theirs, w_raw, w_flat,
                  ids_send, ids_recv, z_send, z_recv, y_send, y_recv, x_send, x_recv, own_sem, w_sem, ids_sem):
    seq, x = lax.axis_index("seq"), lax.axis_index("mp")
    nx = lax.axis_size("mp")
    z, y, c = seq // (ny * CORES), (seq // CORES) % ny, seq % CORES
    half = x % 2
    nr = ny * CORES
    right, left = (seq, (x + 1) % nx), (seq, (x + nx - 1) % nx)

    def along_z(k):
        return (((z + k) % nz * ny + y) * CORES + c, x)

    def in_row(r):
        return ((z * ny + (y + r % ny) % ny) * CORES + (c + r // ny) % CORES, x)

    def in_row_back(r):
        return ((z * ny + (y + ny - r % ny) % ny) * CORES + (c + r // ny) % CORES, x)

    ids_load = pltpu.make_async_copy(ids_hbm, ids_ref, ids_sem)
    ids_load.start()
    barrier = pltpu.get_barrier_semaphore()
    for k in (1, nz - 1, 2, nz - 2, nz // 2):
        pl.semaphore_signal(barrier, inc=1, device_id=along_z(k), device_id_type=MESH)
    for r in range(1, nr):
        pl.semaphore_signal(barrier, inc=1, device_id=in_row(r), device_id_type=MESH)
    for to in (right, left):
        pl.semaphore_signal(barrier, inc=1, device_id=to, device_id_type=MESH)
    own_copy = pltpu.make_async_copy(enc_ref.at[:, half], pool.at[0], own_sem)
    own_copy.start()
    w_copy = pltpu.make_async_copy(w_ref, w_raw, w_sem)
    w_copy.start()
    ids_load.wait()
    pl.semaphore_wait(barrier, 5 + (nr - 1) + 2)

    def ids_copy(r):
        return pltpu.make_async_remote_copy(ids_ref, ids_in.at[r], ids_send.at[r], ids_recv.at[r],
                                            device_id=in_row_back(r), device_id_type=MESH)

    def z_copy(step):
        k = step_distance(step, nz)
        return pltpu.make_async_remote_copy(enc_ref.at[:, half], pool.at[step], z_send.at[step], z_recv.at[step],
                                            device_id=along_z(k), device_id_type=MESH)

    def pass_on(step):
        return pltpu.make_async_remote_copy(pool.at[step], pool.at[step + 3], z_send.at[step + 3], z_recv.at[step + 3],
                                            device_id=along_z(jnp.where(step == 3, 1, nz - 1)), device_id_type=MESH)

    def y_copy(step, r):
        return pltpu.make_async_remote_copy(picked.at[step, r], mine.at[step, r], y_send.at[step, r],
                                            y_recv.at[step, r], device_id=in_row(r), device_id_type=MESH)

    def x_copy(step, d):
        at = pl.ds(d * ny, ny)
        return pltpu.make_async_remote_copy(mine.at[step, at], theirs.at[step, at], x_send.at[step, d], x_recv.at[step, d],
                                            device_id=(right, left)[d], device_id_type=MESH)

    for r in range(1, nr):
        ids_copy(r).start()
    for step in range(1, 6):
        z_copy(step).start()

    w_copy.wait()
    kinds = w_flat.shape[1] // 128
    per = 256 // kinds
    out_row = lax.broadcasted_iota(jnp.int32, (256, 256), 0)
    in_col = lax.broadcasted_iota(jnp.int32, (256, 256), 1)
    order = jnp.where(in_col == out_row % per * kinds + out_row // per, 1.0, 0.0).astype(jnp.bfloat16)

    def unweave(i, _):
        for u in range(8):
            b = i * 8 + u
            block = w_raw[pl.ds(pl.multiple_of(b * 256, 256), 256), :]
            sorted_rows = jnp.dot(order, block, preferred_element_type=jnp.float32).astype(jnp.bfloat16)
            for kind in range(kinds):
                at = (kind % 2) * (kinds // 2) + kind // 2
                w_flat[pl.ds(pl.multiple_of(b * per, per), per), at * 128:at * 128 + 128] = sorted_rows[kind * per:(kind + 1) * per]
        return 0

    lax.fori_loop(0, w_raw.shape[0] // 2048, unweave, 0)

    steps = lax.broadcasted_iota(jnp.int32, (nz, 1), 0)
    owner = ((z + nz - step_distance(steps, nz)) % nz * ny + y) * CORES + c
    for r in range(nr):
        if r > 0:
            ids_copy(r).wait_recv()
        ids = ids_ref[...] if r == 0 else ids_in[r]
        for t in range(TILES):
            hit = (ids[0:1] == owner * TILES + t) | (ids[1:2] == owner * TILES + t)
            count = jnp.sum(jnp.where(hit, 1.0, 0.0), axis=1, keepdims=True)
            sel[r, t] = jnp.broadcast_to(count, (nz, 128))

    def pick(step):
        width = pool.shape[-1] // 128
        tiles = [pool[step, t] for t in range(TILES)]
        for r in range(nr):
            total = None
            for t in range(TILES):
                lane = jnp.broadcast_to(sel[r, t, pl.ds(step, 1), :], (16, 128)).astype(jnp.bfloat16)
                term = tiles[t] * jnp.concatenate([lane] * width, axis=1)
                total = term if total is None else total + term
            if r == 0:
                mine[step, 0] = total
            else:
                picked[step, r] = total
                y_copy(step, r).start()

    own_copy.wait()
    pick(0)

    def project(step, part, first):
        flat = part[step].reshape(nr * 16, part.shape[-1])
        span = w_flat.shape[1] // 2

        def columns(i, _):
            at = pl.ds(pl.multiple_of(i * span, span), span)
            out = jnp.dot(flat, w_flat[:, at], preferred_element_type=jnp.float32).astype(jnp.bfloat16)
            kv_ref[pl.ds(step * nr, nr), first:first + 16, at] = out.reshape(nr, 16, span)
            return 0

        lax.fori_loop(0, 2, columns, 0)

    def body(i, _):
        @pl.when(i < nz)
        def _():
            z_copy(i).wait_recv()

            @pl.when((i == 3) | (i == 4))
            def _():
                pass_on(i).start()

            pick(i)

        @pl.when((i >= X_LAG) & (i < nz + X_LAG))
        def _():
            for d in range(2):
                for r in range(d * ny, (d + 1) * ny):
                    if r > 0:
                        y_copy(i - X_LAG, r).wait_recv()
                x_copy(i - X_LAG, d).start()
            project(i - X_LAG, mine, 0)

        @pl.when(i >= P_LAG)
        def _():
            for d in range(2):
                x_copy(i - P_LAG, d).wait_recv()
            project(i - P_LAG, theirs, 16)

        return 0

    lax.fori_loop(1, nz + P_LAG, body, 0)

    for r in range(1, nr):
        ids_copy(r).wait_send()

    def drain(step, _):
        @pl.when(step > 0)
        def _():
            z_copy(step).wait_send()

        for r in range(1, nr):
            y_copy(step, r).wait_send()
        for d in range(2):
            x_copy(step, d).wait_send()
        return 0

    lax.fori_loop(0, nz, drain, 0)


def gather_and_project(ids, encoded, weights, nz, ny):
    rows, width = 2 * encoded.shape[2], encoded.shape[3]
    nr = ny * CORES
    features = weights.shape[0] * 128 // width
    dma = pltpu.SemaphoreType.DMA
    hbm = pl.BlockSpec(memory_space=pltpu.HBM)
    bf16 = jnp.bfloat16
    slots = nz * nr
    return pl.pallas_call(
        functools.partial(gather_kernel, nz, ny),
        out_shape=jax.ShapeDtypeStruct((slots, rows, features), bf16),
        in_specs=[hbm, hbm, hbm],
        out_specs=pl.BlockSpec(memory_space=pltpu.VMEM),
        scratch_shapes=[
            pltpu.VMEM(ids.shape, jnp.int32),
            pltpu.VMEM((nr,) + ids.shape, jnp.int32),
            pltpu.VMEM((nr, TILES, nz, 128), jnp.float32),
            pltpu.VMEM((nz, TILES, 16, width), bf16),
            pltpu.VMEM((nz, nr, 16, width), bf16),
            pltpu.VMEM((nz, nr, 16, width), bf16),
            pltpu.VMEM((nz, nr, 16, width), bf16),
            pltpu.VMEM(weights.shape, bf16),
            pltpu.VMEM((width, features), bf16),
            dma((nr,)), dma((nr,)), dma((nz,)), dma((nz,)), dma((nz, nr)), dma((nz, nr)), dma((nz, 2)), dma((nz, 2)),
            dma, dma, dma,
        ],
        compiler_params=pltpu.CompilerParams(collective_id=0, has_side_effects=True, vmem_limit_bytes=20 << 20),
        cost_estimate=pl.CostEstimate(flops=2 * slots * rows * width * features, bytes_accessed=16 << 20, transcendentals=0),
    )(ids, encoded, weights)


def attend_kernel(chunk, nz, ny, ids_ref, q, kv, o_hbm, o, o_sem):
    groups = q.shape[0] // GROUP
    chunks = groups // chunk
    width = q.shape[1]
    span = chunk * GROUP

    def o_copy(i):
        at = pl.ds(i * span, span)
        return pltpu.make_async_copy(o.at[at], o_hbm.at[at], o_sem.at[i])

    seq = lax.axis_index("seq")
    z, y, c = seq // (ny * CORES), (seq // CORES) % ny, seq % CORES

    def slot_of(tile):
        owner = tile // TILES
        k = (z + nz - owner // (ny * CORES)) % nz
        return (distance_step(k, nz) * CORES + (c + owner) % CORES) * ny + (y + ny - owner // CORES % ny) % ny

    zero = jnp.zeros((GROUP, HEAD_DIM), jnp.bfloat16)

    def step(i, _):
        slots = [[slot_of(ids_ref[j, i * chunk + u]) for j in range(2)] for u in range(chunk)]
        rows = [pl.ds(pl.multiple_of((i * chunk + u) * GROUP, GROUP), GROUP) for u in range(chunk)]
        units = [(u, h * 256) for u in range(chunk) for h in range(width // 256)]

        def tile_rows(u, at):
            return jnp.concatenate([kv[slot, :, at:at + 256] for slot in slots[u]], 0)

        all_scores = []
        for u, at in units:
            qh = q[rows[u], at:at + 256]
            q2 = jnp.concatenate([jnp.concatenate([qh[:, :128], zero], 1), jnp.concatenate([zero, qh[:, 128:]], 1)], 0)
            all_scores.append(lax.dot_general(tile_rows(u, at), q2, (((1,), (1,)), ((), ())), preferred_element_type=jnp.float32))
        all_probs = []
        for scores in all_scores:
            top = jnp.max(scores, axis=0, keepdims=True)
            expd = jnp.exp2((scores - top) * SCALE)
            all_probs.append((expd * (1.0 / jnp.sum(expd, axis=0, keepdims=True))).astype(jnp.bfloat16))
        for (u, at), probs in zip(units, all_probs):
            mixed = lax.dot_general(probs, tile_rows(u, width + at), (((0,), (0,)), ((), ())), preferred_element_type=jnp.float32)
            o[rows[u], at:at + 256] = jnp.concatenate([mixed[:GROUP, :128], mixed[GROUP:, 128:]], 1).astype(jnp.bfloat16)
        o_copy(i).start()
        return 0

    lax.fori_loop(0, chunks, step, 0)
    for i in range(chunks):
        o_copy(i).wait()


def attend(ids, queries, kv, nz, ny, chunk=8):
    chunks = queries.shape[0] // GROUP // chunk
    vmem = pl.BlockSpec(memory_space=pltpu.VMEM)
    hbm = pl.BlockSpec(memory_space=pltpu.HBM)
    dma = pltpu.SemaphoreType.DMA
    return pl.pallas_call(
        functools.partial(attend_kernel, chunk, nz, ny),
        out_shape=jax.ShapeDtypeStruct(queries.shape, queries.dtype),
        in_specs=[pl.BlockSpec(memory_space=pltpu.SMEM), vmem, vmem],
        out_specs=hbm,
        scratch_shapes=[pltpu.VMEM(queries.shape, jnp.bfloat16), dma((chunks,))],
        compiler_params=pltpu.CompilerParams(vmem_limit_bytes=20 << 20),
        cost_estimate=pl.CostEstimate(flops=4 * queries.size * GROUP, bytes_accessed=17 << 20, transcendentals=queries.size // 2),
    )(ids, queries, kv)


def body(ny, queries, encoded, w_kv, retrieved):
    nz = lax.axis_size("seq") // (ny * CORES)
    inner, _, width = w_kv.shape
    weights = w_kv.reshape(inner, 2, width // 128, 128).transpose(0, 2, 1, 3).reshape(-1, 128)
    in_hbm = functools.partial(pltpu.with_memory_space_constraint, memory_space=pltpu.HBM)
    ids = in_hbm(retrieved.T)
    kv = gather_and_project(ids, in_hbm(encoded.reshape(encoded.shape[0], 2, -1, inner)), in_hbm(weights), nz, ny)
    return attend(ids, queries, kv, nz, ny)


def solution(mesh):
    in_specs = (P("seq", "mp"), P("seq", None, None), P(None, None, "mp"), P("seq", None))
    return jax.shard_map(functools.partial(body, 4), mesh=mesh, in_specs=in_specs, out_specs=P("seq", "mp"), check_vma=False)
```

```python
import functools

import jax
import jax.numpy as jnp
from jax import lax
from jax.experimental import pallas as pl
from jax.experimental.pallas import tpu as pltpu
from jax.sharding import PartitionSpec as P

GROUP = 64
HEAD_DIM = 128
TILES = 4
CORES = 2
MESH = pl.DeviceIdType.MESH
X_LAG, P_LAG = 2, 4
SCALE = (HEAD_DIM ** -0.5) * 1.4426950408889634


def step_distance(step, nz):
    near = jnp.where(step % 2 == 1, (step + 1) // 2, (nz - step // 2) % nz)
    return jnp.where(step < 5, near, jnp.where(step == 5, nz // 2, jnp.where(step == 6, 3, nz - 3)))


def distance_step(k, nz):
    near = jnp.where(k == 0, 0, jnp.where(k <= 2, 2 * k - 1, 2 * (nz - k)))
    return jnp.where(k == nz // 2, 5, jnp.where(k == 3, 6, jnp.where(k == nz - 3, 7, near)))


def gather_kernel(nz, ny, ids_hbm, enc_ref, w_ref, kv_ref,
                  ids_ref, ids_in, sel, pool, picked, mine, theirs, w_raw, w_flat,
                  ids_send, ids_recv, z_send, z_recv, y_send, y_recv, x_send, x_recv, own_sem, w_sem, ids_sem):
    seq, x = lax.axis_index("seq"), lax.axis_index("mp")
    nx = lax.axis_size("mp")
    z, y, c = seq // (ny * CORES), (seq // CORES) % ny, seq % CORES
    half = x % 2
    nr = ny * CORES
    right, left = (seq, (x + 1) % nx), (seq, (x + nx - 1) % nx)

    def along_z(k):
        return (((z + k) % nz * ny + y) * CORES + c, x)

    def in_row(r):
        return ((z * ny + (y + r % ny) % ny) * CORES + (c + r // ny) % CORES, x)

    def in_row_back(r):
        return ((z * ny + (y + ny - r % ny) % ny) * CORES + (c + r // ny) % CORES, x)

    ids_load = pltpu.make_async_copy(ids_hbm, ids_ref, ids_sem)
    ids_load.start()
    barrier = pltpu.get_barrier_semaphore()
    for k in (1, nz - 1, 2, nz - 2, nz // 2):
        pl.semaphore_signal(barrier, inc=1, device_id=along_z(k), device_id_type=MESH)
    for r in range(1, nr):
        pl.semaphore_signal(barrier, inc=1, device_id=in_row(r), device_id_type=MESH)
    for to in (right, left):
        pl.semaphore_signal(barrier, inc=1, device_id=to, device_id_type=MESH)
    own_copy = pltpu.make_async_copy(enc_ref.at[:, half], pool.at[0], own_sem)
    own_copy.start()
    w_copy = pltpu.make_async_copy(w_ref, w_raw, w_sem)
    w_copy.start()
    ids_load.wait()
    pl.semaphore_wait(barrier, 5 + (nr - 1) + 2)

    def ids_copy(r):
        return pltpu.make_async_remote_copy(ids_ref, ids_in.at[r], ids_send.at[r], ids_recv.at[r],
                                            device_id=in_row_back(r), device_id_type=MESH)

    def z_copy(step):
        k = step_distance(step, nz)
        return pltpu.make_async_remote_copy(enc_ref.at[:, half], pool.at[step], z_send.at[step], z_recv.at[step],
                                            device_id=along_z(k), device_id_type=MESH)

    def pass_on(step):
        return pltpu.make_async_remote_copy(pool.at[step], pool.at[step + 3], z_send.at[step + 3], z_recv.at[step + 3],
                                            device_id=along_z(jnp.where(step == 3, 1, nz - 1)), device_id_type=MESH)

    def y_copy(step, r):
        return pltpu.make_async_remote_copy(picked.at[step, r], mine.at[step, r], y_send.at[step, r],
                                            y_recv.at[step, r], device_id=in_row(r), device_id_type=MESH)

    def x_copy(step, d):
        at = pl.ds(d * ny + 1, ny - 1) if d < 2 else pl.ds((d - 2) * ny, 1)
        return pltpu.make_async_remote_copy(mine.at[step, at], theirs.at[step, at], x_send.at[step, d], x_recv.at[step, d],
                                            device_id=(right, left)[d % 2], device_id_type=MESH)

    for r in range(1, nr):
        ids_copy(r).start()
    for step in range(1, 6):
        z_copy(step).start()

    w_copy.wait()
    kinds = w_flat.shape[1] // 128
    per = 256 // kinds
    out_row = lax.broadcasted_iota(jnp.int32, (256, 256), 0)
    in_col = lax.broadcasted_iota(jnp.int32, (256, 256), 1)
    order = jnp.where(in_col == out_row % per * kinds + out_row // per, 1.0, 0.0).astype(jnp.bfloat16)

    def unweave(i, _):
        for u in range(8):
            b = i * 8 + u
            block = w_raw[pl.ds(pl.multiple_of(b * 256, 256), 256), :]
            sorted_rows = jnp.dot(order, block, preferred_element_type=jnp.float32).astype(jnp.bfloat16)
            for kind in range(kinds):
                at = (kind % 2) * (kinds // 2) + kind // 2
                w_flat[pl.ds(pl.multiple_of(b * per, per), per), at * 128:at * 128 + 128] = sorted_rows[kind * per:(kind + 1) * per]
        return 0

    lax.fori_loop(0, w_raw.shape[0] // 2048, unweave, 0)

    steps = lax.broadcasted_iota(jnp.int32, (nz, 1), 0)
    owner = ((z + nz - step_distance(steps, nz)) % nz * ny + y) * CORES + c
    for r in range(nr):
        if r > 0:
            ids_copy(r).wait_recv()
        ids = ids_ref[...] if r == 0 else ids_in[r]
        for t in range(TILES):
            hit = (ids[0:1] == owner * TILES + t) | (ids[1:2] == owner * TILES + t)
            count = jnp.sum(jnp.where(hit, 1.0, 0.0), axis=1, keepdims=True)
            sel[r, t] = jnp.broadcast_to(count, (nz, 128))

    def pick(step):
        width = pool.shape[-1] // 128
        tiles = [pool[step, t] for t in range(TILES)]
        for r in range(nr):
            total = None
            for t in range(TILES):
                lane = jnp.broadcast_to(sel[r, t, pl.ds(step, 1), :], (16, 128)).astype(jnp.bfloat16)
                term = tiles[t] * jnp.concatenate([lane] * width, axis=1)
                total = term if total is None else total + term
            if r == 0:
                mine[step, 0] = total
                x_copy(step, 2).start()
            else:
                picked[step, r] = total
                y_copy(step, r).start()

    own_copy.wait()
    pick(0)

    def project(step, part, first):
        flat = part[step].reshape(nr * 16, part.shape[-1])
        span = w_flat.shape[1] // 2

        def columns(i, _):
            at = pl.ds(pl.multiple_of(i * span, span), span)
            out = jnp.dot(flat, w_flat[:, at], preferred_element_type=jnp.float32).astype(jnp.bfloat16)
            kv_ref[pl.ds(step * nr, nr), first:first + 16, at] = out.reshape(nr, 16, span)
            return 0

        lax.fori_loop(0, 2, columns, 0)

    def body(i, _):
        @pl.when(i < nz)
        def _():
            z_copy(i).wait_recv()

            @pl.when((i == 3) | (i == 4))
            def _():
                pass_on(i).start()

            pick(i)

        @pl.when(i <= nz)
        def _():
            y_copy(i - 1, ny).wait_recv()
            x_copy(i - 1, 3).start()

        @pl.when((i >= X_LAG) & (i < nz + X_LAG))
        def _():
            for d in range(2):
                for r in range(d * ny, (d + 1) * ny):
                    if r % ny > 0:
                        y_copy(i - X_LAG, r).wait_recv()
                x_copy(i - X_LAG, d).start()
            project(i - X_LAG, mine, 0)

        @pl.when(i >= P_LAG)
        def _():
            for d in range(4):
                x_copy(i - P_LAG, d).wait_recv()
            project(i - P_LAG, theirs, 16)

        return 0

    lax.fori_loop(1, nz + P_LAG, body, 0)

    for r in range(1, nr):
        ids_copy(r).wait_send()

    def drain(step, _):
        @pl.when(step > 0)
        def _():
            z_copy(step).wait_send()

        for r in range(1, nr):
            y_copy(step, r).wait_send()
        for d in range(4):
            x_copy(step, d).wait_send()
        return 0

    lax.fori_loop(0, nz, drain, 0)


def gather_and_project(ids, encoded, weights, nz, ny):
    rows, width = 2 * encoded.shape[2], encoded.shape[3]
    nr = ny * CORES
    features = weights.shape[0] * 128 // width
    dma = pltpu.SemaphoreType.DMA
    hbm = pl.BlockSpec(memory_space=pltpu.HBM)
    bf16 = jnp.bfloat16
    slots = nz * nr
    return pl.pallas_call(
        functools.partial(gather_kernel, nz, ny),
        out_shape=jax.ShapeDtypeStruct((slots, rows, features), bf16),
        in_specs=[hbm, hbm, hbm],
        out_specs=pl.BlockSpec(memory_space=pltpu.VMEM),
        scratch_shapes=[
            pltpu.VMEM(ids.shape, jnp.int32),
            pltpu.VMEM((nr,) + ids.shape, jnp.int32),
            pltpu.VMEM((nr, TILES, nz, 128), jnp.float32),
            pltpu.VMEM((nz, TILES, 16, width), bf16),
            pltpu.VMEM((nz, nr, 16, width), bf16),
            pltpu.VMEM((nz, nr, 16, width), bf16),
            pltpu.VMEM((nz, nr, 16, width), bf16),
            pltpu.VMEM(weights.shape, bf16),
            pltpu.VMEM((width, features), bf16),
            dma((nr,)), dma((nr,)), dma((nz,)), dma((nz,)), dma((nz, nr)), dma((nz, nr)), dma((nz, 4)), dma((nz, 4)),
            dma, dma, dma,
        ],
        compiler_params=pltpu.CompilerParams(collective_id=0, has_side_effects=True, vmem_limit_bytes=20 << 20),
        cost_estimate=pl.CostEstimate(flops=2 * slots * rows * width * features, bytes_accessed=16 << 20, transcendentals=0),
    )(ids, encoded, weights)


def attend_kernel(chunk, nz, ny, ids_ref, q, kv, o_hbm, o, o_sem):
    groups = q.shape[0] // GROUP
    chunks = groups // chunk
    width = q.shape[1]
    span = chunk * GROUP

    def o_copy(i):
        at = pl.ds(i * span, span)
        return pltpu.make_async_copy(o.at[at], o_hbm.at[at], o_sem.at[i])

    seq = lax.axis_index("seq")
    z, y, c = seq // (ny * CORES), (seq // CORES) % ny, seq % CORES

    def slot_of(tile):
        owner = tile // TILES
        k = (z + nz - owner // (ny * CORES)) % nz
        return (distance_step(k, nz) * CORES + (c + owner) % CORES) * ny + (y + ny - owner // CORES % ny) % ny

    zero = jnp.zeros((GROUP, HEAD_DIM), jnp.bfloat16)

    def step(i, _):
        slots = [[slot_of(ids_ref[j, i * chunk + u]) for j in range(2)] for u in range(chunk)]
        rows = [pl.ds(pl.multiple_of((i * chunk + u) * GROUP, GROUP), GROUP) for u in range(chunk)]
        units = [(u, h * 256) for u in range(chunk) for h in range(width // 256)]

        def tile_rows(u, at):
            return jnp.concatenate([kv[slot, :, at:at + 256] for slot in slots[u]], 0)

        all_scores = []
        for u, at in units:
            qh = q[rows[u], at:at + 256]
            q2 = jnp.concatenate([jnp.concatenate([qh[:, :128], zero], 1), jnp.concatenate([zero, qh[:, 128:]], 1)], 0)
            all_scores.append(lax.dot_general(tile_rows(u, at), q2, (((1,), (1,)), ((), ())), preferred_element_type=jnp.float32))
        all_probs = []
        for scores in all_scores:
            top = jnp.max(scores, axis=0, keepdims=True)
            expd = jnp.exp2((scores - top) * SCALE)
            all_probs.append((expd * (1.0 / jnp.sum(expd, axis=0, keepdims=True))).astype(jnp.bfloat16))
        for (u, at), probs in zip(units, all_probs):
            mixed = lax.dot_general(probs, tile_rows(u, width + at), (((0,), (0,)), ((), ())), preferred_element_type=jnp.float32)
            o[rows[u], at:at + 256] = jnp.concatenate([mixed[:GROUP, :128], mixed[GROUP:, 128:]], 1).astype(jnp.bfloat16)
        o_copy(i).start()
        return 0

    lax.fori_loop(0, chunks, step, 0)
    for i in range(chunks):
        o_copy(i).wait()


def attend(ids, queries, kv, nz, ny, chunk=8):
    chunks = queries.shape[0] // GROUP // chunk
    vmem = pl.BlockSpec(memory_space=pltpu.VMEM)
    hbm = pl.BlockSpec(memory_space=pltpu.HBM)
    dma = pltpu.SemaphoreType.DMA
    return pl.pallas_call(
        functools.partial(attend_kernel, chunk, nz, ny),
        out_shape=jax.ShapeDtypeStruct(queries.shape, queries.dtype),
        in_specs=[pl.BlockSpec(memory_space=pltpu.SMEM), vmem, vmem],
        out_specs=hbm,
        scratch_shapes=[pltpu.VMEM(queries.shape, jnp.bfloat16), dma((chunks,))],
        compiler_params=pltpu.CompilerParams(vmem_limit_bytes=20 << 20),
        cost_estimate=pl.CostEstimate(flops=4 * queries.size * GROUP, bytes_accessed=17 << 20, transcendentals=queries.size // 2),
    )(ids, queries, kv)


def body(ny, queries, encoded, w_kv, retrieved):
    nz = lax.axis_size("seq") // (ny * CORES)
    inner, _, width = w_kv.shape
    weights = w_kv.reshape(inner, 2, width // 128, 128).transpose(0, 2, 1, 3).reshape(-1, 128)
    in_hbm = functools.partial(pltpu.with_memory_space_constraint, memory_space=pltpu.HBM)
    ids = in_hbm(retrieved.T)
    kv = gather_and_project(ids, in_hbm(encoded.reshape(encoded.shape[0], 2, -1, inner)), in_hbm(weights), nz, ny)
    return attend(ids, queries, kv, nz, ny)


def solution(mesh):
    in_specs = (P("seq", "mp"), P("seq", None, None), P(None, None, "mp"), P("seq", None))
    return jax.shard_map(functools.partial(body, 4), mesh=mesh, in_specs=in_specs, out_specs=P("seq", "mp"), check_vma=False)
```
